32 devices in a mesh: section: 4 (over z), head: 8 (over y, x, core).
Axes of the slice: x: 2, y: 2, z: 4, core: 2. Of those that a mesh axis runs over, the one named last changes fastest.
Arguments:
- section_inputs: bfloat16 [4, 256, 1024], P('section'), may hold values from -6 to 6
- section_cotangents: bfloat16 [4, 256, 1024], P('section'), may hold values from -6 to 6
- fresh_tokens: bfloat16 [2, 256, 1024], replicated, may hold values from -6 to 6
- fresh_cotangents: bfloat16 [2, 256, 1024], replicated, may hold values from -6 to 6
- norm_gain: float32 [4, 1024], P('section'), may hold values from 0.1 to 1.9
- query_weight: bfloat16 [4, 1024, 16384], P('section', None, 'head'), as said below
- key_weight: bfloat16 [4, 1024, 16384], P('section', None, 'head'), may hold values from -0.1875 to 0.1875
- value_weight: bfloat16 [4, 1024, 16384], P('section', None, 'head'), may hold values from -0.1875 to 0.1875
- out_weight: bfloat16 [4, 16384, 1024], P('section', 'head'), may hold values from -0.1875 to 0.1875
- saved_inputs: bfloat16 [4, 4, 256, 1024], P('section', None, None, 'head'), may hold values from -6 to 6
- reload_slot: int32 [2, 4], replicated, may hold values from 0 to 3
Outputs:
- next_inputs: bfloat16 [4, 256, 1024], P('section')
- next_cotangents: bfloat16 [4, 256, 1024], P('section')
- saved_after: bfloat16 [4, 4, 256, 1024], P('section', None, None, 'head')
- query_grad: bfloat16 [4, 1024, 16384], P('section', None, 'head')
- key_grad: bfloat16 [4, 1024, 16384], P('section', None, 'head')
- value_grad: bfloat16 [4, 1024, 16384], P('section', None, 'head')
- out_grad: bfloat16 [4, 16384, 1024], P('section', 'head')
- gain_grad: float32 [4, 1024], P('section', 'head')
The draws below stay inside these ranges and needn't reach their ends.
Inputs may be any that keep to these rules, and one draw needn't show every extreme that they name: `query_weight`: independent entries.
All inputs are finite; a program needn't handle non-finite values.
Results may differ from the reference program's by a relative error of at most 0.015.
The reference program's roundings to bfloat16 on the way count: a program that leaves them out, or rounds other values in their place, can miss the bound.
Values may be sent and summed in bfloat16 or wider, within the bound.
A program may use at most 128 MiB of HBM per device.

```python
import math
import jax
import jax.numpy as jnp
from jax import lax

D = 1024
HEADS = 128
DK = 128
MB = 256
SLOTS = 4
TICKS = 2
SECTIONS = 4


def draw_query_weight(key, part):
    base = jax.random.normal(jax.random.fold_in(key, 11), (SECTIONS, D, HEADS * DK), jnp.float32) / math.sqrt(D)
    return base.astype(jnp.bfloat16)


def place_ends(drawn, key, low, largest):
    shape = drawn.shape
    index_at = [jax.random.randint(jax.random.fold_in(key, axis), (), 0, shape[axis]) for axis in range(len(shape))]
    drawn = drawn.at[tuple(index_at)].set(low)
    longest = shape.index(max(shape))
    index_at[longest] = (index_at[longest] + 1) % shape[longest]
    return drawn.at[tuple(index_at)].set(largest)


def block_levels(own_key, extent, pieces, least, largest):
    gain = 1.0
    for dim, blocks in pieces:
        draws = jax.random.uniform(jax.random.fold_in(jax.random.fold_in(own_key, 6), dim), (blocks,), jnp.float32, least / len(pieces), largest / len(pieces))
        gain = gain * jnp.repeat(jnp.exp(draws), extent[dim] // blocks).reshape((-1,) + (1,) * (len(extent) - 1 - dim))
    return gain


def gaussian(rng, shape, width, most, pieces=(), kind=jnp.bfloat16):
    values = width * jax.random.normal(rng, shape, jnp.float32)
    if pieces:
        values = values * block_levels(rng, shape, pieces, -0.22, 0.18)
    return jnp.clip(values, -most, most).astype(kind)


def setup_inputs(seed: int = 0) -> dict:
    arg_keys = jax.random.split(jax.random.key(seed), 12)
    section_inputs = gaussian(arg_keys[0], (SECTIONS, MB, D), 1.0, 6.0, ((0, 4),))
    section_cotangents = gaussian(arg_keys[1], (SECTIONS, MB, D), 1.0, 6.0, ((0, 4),))
    fresh_tokens = gaussian(arg_keys[2], (TICKS, MB, D), 1.0, 6.0)
    fresh_cotangents = gaussian(arg_keys[3], (TICKS, MB, D), 1.0, 6.0)
    norm_gain = jnp.clip(1.0 + 0.18 * jax.random.normal(arg_keys[4], (SECTIONS, D), jnp.float32), 0.1, 1.9)
    query_weight = draw_query_weight(jax.random.fold_in(arg_keys[11], 71), 0)
    key_weight = gaussian(arg_keys[6], (SECTIONS, D, HEADS * DK), D ** -0.5, 0.1875, ((0, 4), (2, 8)))
    value_weight = gaussian(arg_keys[7], (SECTIONS, D, HEADS * DK), D ** -0.5, 0.1875, ((0, 4), (2, 8)))
    out_weight = gaussian(arg_keys[8], (SECTIONS, HEADS * DK, D), (HEADS * DK // 16) ** -0.5, 0.1875, ((0, 4), (1, 8)))
    saved_inputs = gaussian(arg_keys[9], (SECTIONS, SLOTS, MB, D), 1.0, 6.0, ((0, 4), (3, 8)))
    reload_slot = place_ends(jax.random.randint(arg_keys[10], (TICKS, SECTIONS), 0, SLOTS), jax.random.fold_in(arg_keys[10], 1), 0, SLOTS - 1).astype(jnp.int32)
    return {"section_inputs": section_inputs, "section_cotangents": section_cotangents, "fresh_tokens": fresh_tokens, "fresh_cotangents": fresh_cotangents, "norm_gain": norm_gain, "query_weight": query_weight, "key_weight": key_weight, "value_weight": value_weight, "out_weight": out_weight, "saved_inputs": saved_inputs, "reload_slot": reload_slot}


epsilon = 1e-06

def normalize(rows, gain_row):
    floats = rows.astype(jnp.float32)
    inverse = lax.rsqrt(lax.optimization_barrier(jnp.mean(floats * floats, axis=-1, keepdims=True)) + epsilon)
    unit_rows = floats * inverse
    return ((unit_rows * gain_row).astype(jnp.bfloat16), unit_rows, inverse)

def split_heads(rows):
    return rows.reshape(rows.shape[0], -1, DK).astype(jnp.float32)

def attend(normed, query_part, key_part, value_part):
    queries = jnp.dot(normed, query_part, preferred_element_type=jnp.float32).astype(jnp.bfloat16)
    key_rows = jnp.dot(normed, key_part, preferred_element_type=jnp.float32).astype(jnp.bfloat16)
    value_rows = jnp.dot(normed, value_part, preferred_element_type=jnp.float32).astype(jnp.bfloat16)
    scores = jnp.einsum('qhd,khd->hqk', split_heads(queries), split_heads(key_rows)) * DK ** (-0.5)
    highest = lax.optimization_barrier(jnp.max(scores, axis=-1, keepdims=True))
    exponent = jnp.exp(scores - highest)
    softmax_rows = exponent / lax.optimization_barrier(jnp.sum(exponent, axis=-1, keepdims=True))
    softmax_low = softmax_rows.astype(jnp.bfloat16)
    context = jnp.einsum('hqk,khd->qhd', softmax_low.astype(jnp.float32), split_heads(value_rows))
    context = context.astype(jnp.bfloat16).reshape(normed.shape[0], -1)
    return (queries, key_rows, value_rows, softmax_rows, softmax_low, context)

def forward_layer(rows, gain_row, query_part, key_part, value_part, out_part):
    normed, unit_rows, inverse = normalize(rows, gain_row)
    context = attend(normed, query_part, key_part, value_part)[5]
    total = rows.astype(jnp.float32) + jnp.dot(context, out_part, preferred_element_type=jnp.float32)
    return total.astype(jnp.bfloat16)

def backward_layer(rows, upstream, gain_row, query_part, key_part, value_part, out_part):
    normed, unit_rows, inverse = normalize(rows, gain_row)
    queries, key_rows, value_rows, softmax_rows, softmax_low, context = attend(normed, query_part, key_part, value_part)
    token_count = rows.shape[0]
    out_term = jnp.dot(context.T, upstream, preferred_element_type=jnp.float32)
    context_grad = jnp.dot(upstream, out_part.T, preferred_element_type=jnp.float32).astype(jnp.bfloat16)
    softmax_grad = jnp.einsum('qhd,khd->hqk', split_heads(context_grad), split_heads(value_rows))
    value_rows_grad = jnp.einsum('hqk,qhd->khd', softmax_low.astype(jnp.float32), split_heads(context_grad))
    value_rows_grad = value_rows_grad.astype(jnp.bfloat16).reshape(token_count, -1)
    inner = lax.optimization_barrier(jnp.sum(softmax_rows * softmax_grad, axis=-1, keepdims=True))
    score_grad = (softmax_rows * (softmax_grad - inner) * DK ** (-0.5)).astype(jnp.bfloat16).astype(jnp.float32)
    queries_grad = jnp.einsum('hqk,khd->qhd', score_grad, split_heads(key_rows)).astype(jnp.bfloat16).reshape(token_count, -1)
    key_rows_grad = jnp.einsum('hqk,qhd->khd', score_grad, split_heads(queries)).astype(jnp.bfloat16).reshape(token_count, -1)
    query_term = jnp.dot(normed.T, queries_grad, preferred_element_type=jnp.float32)
    key_term = jnp.dot(normed.T, key_rows_grad, preferred_element_type=jnp.float32)
    value_term = jnp.dot(normed.T, value_rows_grad, preferred_element_type=jnp.float32)
    normed_grad = jnp.dot(queries_grad, query_part.T, preferred_element_type=jnp.float32)
    normed_grad = normed_grad + jnp.dot(key_rows_grad, key_part.T, preferred_element_type=jnp.float32)
    normed_grad = normed_grad + jnp.dot(value_rows_grad, value_part.T, preferred_element_type=jnp.float32)
    gain_term = lax.optimization_barrier(jnp.sum(normed_grad * unit_rows, axis=0))
    unit_grad = normed_grad * gain_row
    along = lax.optimization_barrier(jnp.mean(unit_grad * unit_rows, axis=-1, keepdims=True))
    returned = (upstream.astype(jnp.float32) + inverse * (unit_grad - unit_rows * along)).astype(jnp.bfloat16)
    return (returned, (query_term, key_term, value_term, out_term, gain_term))

def reference(section_inputs, section_cotangents, fresh_tokens, fresh_cotangents, norm_gain, query_weight, key_weight, value_weight, out_weight, saved_inputs, reload_slot):
    count = section_inputs.shape[0]
    stores = [saved_inputs[number] for number in range(count)]
    produced = [[None] * TICKS for number in range(count)]
    loaded = [[None] * TICKS for number in range(count)]
    for section_number in range(count):
        row_store = stores[count - 1 - section_number]
        for tick_number in range(TICKS):
            if tick_number == 0:
                current = section_inputs[section_number]
            elif section_number == 0:
                current = fresh_tokens[tick_number - 1]
            else:
                current = produced[section_number - 1][tick_number - 1]
            slot = reload_slot[tick_number, section_number]
            loaded[section_number][tick_number] = lax.dynamic_index_in_dim(row_store, slot, 0, keepdims=False)
            row_store = lax.dynamic_update_index_in_dim(row_store, current, slot, 0)
            produced[section_number][tick_number] = forward_layer(current, norm_gain[section_number], query_weight[section_number], key_weight[section_number], value_weight[section_number], out_weight[section_number])
        stores[count - 1 - section_number] = row_store
    returned = [[None] * TICKS for number in range(count)]
    grads = [None] * count
    for section_number in range(count - 1, -1, -1):
        sums = None
        for tick_number in range(TICKS):
            if tick_number == 0:
                upstream = section_cotangents[section_number]
            elif section_number == count - 1:
                upstream = fresh_cotangents[tick_number - 1]
            else:
                upstream = returned[section_number + 1][tick_number - 1]
            result, terms = backward_layer(loaded[section_number][tick_number], upstream, norm_gain[section_number], query_weight[section_number], key_weight[section_number], value_weight[section_number], out_weight[section_number])
            returned[section_number][tick_number] = result
            sums = terms if sums is None else tuple((a + b for a, b in zip(sums, terms)))
        grads[section_number] = sums
    next_inputs = jnp.stack([fresh_tokens[TICKS - 1]] + [produced[number - 1][TICKS - 1] for number in range(1, count)])
    next_cotangents = jnp.stack([returned[number + 1][TICKS - 1] for number in range(count - 1)] + [fresh_cotangents[TICKS - 1]])
    saved_after = jnp.stack(stores)
    query_grad = jnp.stack([grads[number][0] for number in range(count)]).astype(jnp.bfloat16)
    key_grad = jnp.stack([grads[number][1] for number in range(count)]).astype(jnp.bfloat16)
    value_grad = jnp.stack([grads[number][2] for number in range(count)]).astype(jnp.bfloat16)
    out_grad = jnp.stack([grads[number][3] for number in range(count)]).astype(jnp.bfloat16)
    gain_grad = jnp.stack([grads[number][4] for number in range(count)])
    return (next_inputs, next_cotangents, saved_after, query_grad, key_grad, value_grad, out_grad, gain_grad)
```

```python
import functools

import jax
import jax.numpy as jnp
from jax import lax
from jax.experimental import pallas as pl
from jax.experimental.pallas import tpu as pltpu
from jax.sharding import PartitionSpec as P

DK = 128
TICKS = 2


epsilon = 1e-06
ONES = (((1,), (1,)), ((), ()))
ZEROS = (((0,), (0,)), ((), ()))


def passed_along(value, axis, by):
    count = lax.axis_size(axis)
    pairs = [(i, i + by) for i in range(count) if 0 <= i + by < count]
    return lax.ppermute(value, axis, pairs)


def mirrored(value, axis):
    count = lax.axis_size(axis)
    return lax.ppermute(value, axis, [(i, count - 1 - i) for i in range(count)])


def normalize(rows, gain_row):
    floats = rows.astype(jnp.float32)
    inverse = lax.rsqrt(jnp.mean(floats * floats, axis=-1, keepdims=True) + epsilon)
    unit_rows = floats * inverse
    return ((unit_rows * gain_row).astype(jnp.bfloat16), unit_rows, inverse)


def dot(a, b, dims=(((1,), (0,)), ((), ()))):
    return lax.dot_general(a, b, dims, preferred_element_type=jnp.float32)


def low_dot(a, b, dims=(((1,), (0,)), ((), ()))):
    return dot(a, b, dims).astype(jnp.bfloat16)


def softmax_of(queries, key_rows):
    scores = dot(queries, key_rows, ONES) * DK ** (-0.5)
    exponent = jnp.exp(scores - jnp.max(scores, axis=-1, keepdims=True))
    return exponent * (1.0 / jnp.sum(exponent, axis=-1, keepdims=True))


def forward_kernel(rows, gain, wq, wk, wv, wo, total, normed):
    step = pl.program_id(0)

    @pl.when(step == 0)
    def _():
        normed[...] = normalize(rows[...], gain[...])[0]
        total[...] = jnp.zeros_like(total)

    n = normed[...]
    queries, key_rows, value_rows = low_dot(n, wq[...]), low_dot(n, wk[...]), low_dot(n, wv[...])
    parts = []
    for start in range(0, queries.shape[1], DK):
        head = slice(start, start + DK)
        soft = softmax_of(queries[:, head], key_rows[:, head]).astype(jnp.bfloat16)
        parts.append(low_dot(soft, value_rows[:, head]))
    total[...] += dot(jnp.concatenate(parts, axis=1), wo[...])


def backward_kernel(rows, upstream, gain, wq, wk, wv, wo, total, normed, ctx, qg, kg, vg):
    step = pl.program_id(0)

    @pl.when(step == 0)
    def _():
        normed[...] = normalize(rows[...], gain[...])[0]
        total[...] = jnp.zeros_like(total)

    n = normed[...]
    queries, key_rows, value_rows = low_dot(n, wq[...]), low_dot(n, wk[...]), low_dot(n, wv[...])
    ctx_grad = low_dot(upstream[...], wo[...], ONES)
    for start in range(0, queries.shape[1], DK):
        head = slice(start, start + DK)
        q, k, v, c = queries[:, head], key_rows[:, head], value_rows[:, head], ctx_grad[:, head]
        soft = softmax_of(q, k)
        soft_low = soft.astype(jnp.bfloat16)
        ctx[:, head] = low_dot(soft_low, v)
        soft_grad = dot(c, v, ONES)
        vg[:, head] = low_dot(soft_low, c, ZEROS)
        inner = jnp.sum(soft * soft_grad, axis=-1, keepdims=True)
        score_grad = (soft * (soft_grad - inner) * DK ** (-0.5)).astype(jnp.bfloat16)
        qg[:, head] = low_dot(score_grad, k)
        kg[:, head] = low_dot(score_grad, q, ZEROS)
    total[...] += (
        dot(qg[...], wq[...], ONES) + dot(kg[...], wk[...], ONES) + dot(vg[...], wv[...], ONES)
    )


def gradient_kernel(
    n0, n1, g0, g1, c0, c1, q0, q1, k0, k1, v0, v1, wq, wk, wv, wo, turned, upstream
):
    @pl.when(pl.program_id(0) == 0)
    def _():
        count = n0.shape[0]
        turned[:, :count] = n0[...].T
        turned[:, count:] = n1[...].T
        upstream[:count] = g0[...]
        upstream[count:] = g1[...]

    def both(first, second):
        return jnp.concatenate([first[...], second[...]], axis=0)

    wq[...] = low_dot(turned[...], both(q0, q1))
    wk[...] = low_dot(turned[...], both(k0, k1))
    wv[...] = low_dot(turned[...], both(v0, v1))
    wo[...] = low_dot(both(c0, c1), upstream[...], ZEROS)


def whole(shape):
    return pl.BlockSpec(shape, lambda i: (0,) * len(shape))


def columns(rows, width):
    return pl.BlockSpec((rows, width), lambda i: (0, i))


def row_blocks(width, columns_):
    return pl.BlockSpec((width, columns_), lambda i: (i, 0))


PARAMS = dict(dimension_semantics=("arbitrary",), vmem_limit_bytes=56 * 2**20)


def weight_specs(depth, width):
    return [columns(depth, width)] * 3 + [row_blocks(width, depth)]


def step_width(inner):
    return 4 * DK if inner % (4 * DK) == 0 else DK


def forward_part(rows, weights):
    count, depth = rows.shape
    inner = weights[1].shape[1]
    width = step_width(inner)
    return pl.pallas_call(
        forward_kernel,
        grid=(inner // width,),
        in_specs=[whole((count, depth)), whole((1, depth))] + weight_specs(depth, width),
        out_specs=whole((count, depth)),
        out_shape=jax.ShapeDtypeStruct((count, depth), jnp.float32),
        scratch_shapes=[pltpu.VMEM((count, depth), jnp.bfloat16)],
        compiler_params=pltpu.CompilerParams(**PARAMS),
        cost_estimate=pl.CostEstimate(
            flops=8 * count * depth * inner + 4 * count * count * inner,
            bytes_accessed=8 * depth * inner,
            transcendentals=count * count * inner // DK,
        ),
    )(rows, *weights)


def backward_part(rows, upstream, weights):
    count, depth = rows.shape
    inner = weights[1].shape[1]
    width = step_width(inner)
    wide = jax.ShapeDtypeStruct((count, inner), jnp.bfloat16)
    return pl.pallas_call(
        backward_kernel,
        grid=(inner // width,),
        in_specs=[whole((count, depth)), whole((count, depth)), whole((1, depth))]
        + weight_specs(depth, width),
        out_specs=[whole((count, depth)), whole((count, depth))] + [columns(count, width)] * 4,
        out_shape=[
            jax.ShapeDtypeStruct((count, depth), jnp.float32),
            jax.ShapeDtypeStruct((count, depth), jnp.bfloat16),
        ]
        + [wide] * 4,
        compiler_params=pltpu.CompilerParams(**PARAMS),
        cost_estimate=pl.CostEstimate(
            flops=14 * count * depth * inner + 12 * count * count * inner,
            bytes_accessed=8 * depth * inner,
            transcendentals=count * count * inner // DK,
        ),
    )(rows, upstream, *weights)


def gradients(first, second, g0, g1):
    n0, c0, q0, k0, v0 = first
    n1, c1, q1, k1, v1 = second
    count, depth = n0.shape
    inner = q0.shape[1]
    width = step_width(inner)
    low = jnp.bfloat16
    return pl.pallas_call(
        gradient_kernel,
        grid=(inner // width,),
        in_specs=[whole((count, depth))] * 4 + [columns(count, width)] * 8,
        out_specs=weight_specs(depth, width),
        out_shape=[jax.ShapeDtypeStruct((depth, inner), low)] * 3
        + [jax.ShapeDtypeStruct((inner, depth), low)],
        scratch_shapes=[
            pltpu.VMEM((depth, 2 * count), low),
            pltpu.VMEM((2 * count, depth), low),
        ],
        compiler_params=pltpu.CompilerParams(**PARAMS),
        cost_estimate=pl.CostEstimate(
            flops=16 * count * depth * inner, bytes_accessed=8 * depth * inner, transcendentals=0
        ),
    )(n0, n1, g0, g1, c0, c1, q0, q1, k0, k1, v0, v1)


def sent_forward(rows, part):
    total = lax.psum(part, "head")
    return passed_along((rows.astype(jnp.float32) + total).astype(jnp.bfloat16), "section", 1)


def sent_back(rows, upstream, gain_row, part):
    normed, unit_rows, inverse = normalize(rows, gain_row)
    normed_grad = lax.psum(part, "head")
    gain_full = jnp.sum(normed_grad * unit_rows, axis=0)
    unit_grad = normed_grad * gain_row
    along = jnp.mean(unit_grad * unit_rows, axis=-1, keepdims=True)
    returned = upstream.astype(jnp.float32) + inverse * (unit_grad - unit_rows * along)
    return passed_along(returned.astype(jnp.bfloat16), "section", -1), gain_full


def per_device(
    section_inputs,
    section_cotangents,
    fresh_tokens,
    fresh_cotangents,
    norm_gain,
    query_weight,
    key_weight,
    value_weight,
    out_weight,
    saved_inputs,
    reload_slot,
):
    section_count = lax.axis_size("section")
    section_index = lax.axis_index("section")
    head_index = lax.axis_index("head")
    mirror_index = section_count - 1 - section_index
    share_width = saved_inputs.shape[3]
    column_start = head_index * share_width
    weights = (norm_gain, query_weight[0], key_weight[0], value_weight[0], out_weight[0])
    x0 = section_inputs[0]
    g0 = section_cotangents[0]
    store = saved_inputs[0]
    count = x0.shape[0]

    def own_share(block):
        return lax.dynamic_slice_in_dim(block, column_start, share_width, 1)

    held = lax.dynamic_index_in_dim(reload_slot, mirror_index, 1, keepdims=False)
    held0 = lax.dynamic_index_in_dim(store, held[0], 0, keepdims=False)
    held1 = lax.dynamic_index_in_dim(store, held[1], 0, keepdims=False)
    own = lax.dynamic_index_in_dim(reload_slot, section_index, 1, keepdims=False)

    travel = mirrored(jnp.concatenate([own_share(x0), held0, held1], axis=0), "section")
    arrived, reloads = travel[:count], travel[count:]
    restored = lax.all_gather(reloads, "head", axis=1, tiled=True)
    b0 = restored[:count]
    b1 = jnp.where(own[0] == own[1], x0, restored[count:])

    part = forward_part(x0, weights)
    x1 = jnp.where(section_index == 0, fresh_tokens[0], sent_forward(x0, part))

    part, *first = backward_part(b0, g0, weights)
    moved, gain0 = sent_back(b0, g0, norm_gain, part)
    g1 = jnp.where(section_index == section_count - 1, fresh_cotangents[0], moved)

    part = forward_part(x1, weights)
    x2 = jnp.where(section_index == 0, fresh_tokens[1], sent_forward(x1, part))
    arrived1 = mirrored(own_share(x1), "section")
    store = lax.dynamic_update_index_in_dim(store, arrived, held[0], 0)
    store = lax.dynamic_update_index_in_dim(store, arrived1, held[1], 0)

    part, *second = backward_part(b1, g1, weights)
    moved, gain1 = sent_back(b1, g1, norm_gain, part)
    g2 = jnp.where(section_index == section_count - 1, fresh_cotangents[1], moved)

    grads = gradients(first, second, g0, g1)
    gain = lax.dynamic_slice_in_dim(gain0 + gain1, column_start, share_width, 0)
    return (x2[None], g2[None], store[None], *(grad[None] for grad in grads), gain[None])


def solution(mesh):
    placed = (
        P("section", None, None),
        P("section", None, None),
        P(),
        P(),
        P("section", None),
        P("section", None, "head"),
        P("section", None, "head"),
        P("section", None, "head"),
        P("section", "head", None),
        P("section", None, None, "head"),
        P(),
    )
    return jax.shard_map(
        per_device,
        mesh=mesh,
        in_specs=placed,
        out_specs=(
            P("section", None, None),
            P("section", None, None),
            P("section", None, None, "head"),
            P("section", None, "head"),
            P("section", None, "head"),
            P("section", None, "head"),
            P("section", "head", None),
            P("section", "head"),
        ),
        check_vma=False,
    )
```

```python
import functools

import jax
import jax.numpy as jnp
from jax import lax
from jax.experimental import pallas as pl
from jax.experimental.pallas import tpu as pltpu
from jax.sharding import PartitionSpec as P

DK = 128
TICKS = 2


epsilon = 1e-06
ONES = (((1,), (1,)), ((), ()))
ZEROS = (((0,), (0,)), ((), ()))


def mirrored(value, axis):
    count = lax.axis_size(axis)
    return lax.ppermute(value, axis, [(i, count - 1 - i) for i in range(count)])


def normalize(rows, gain_row):
    floats = rows.astype(jnp.float32)
    inverse = lax.rsqrt(jnp.mean(floats * floats, axis=-1, keepdims=True) + epsilon)
    unit_rows = floats * inverse
    return ((unit_rows * gain_row).astype(jnp.bfloat16), unit_rows, inverse)


def dot(a, b, dims=(((1,), (0,)), ((), ()))):
    return lax.dot_general(a, b, dims, preferred_element_type=jnp.float32)


def low_dot(a, b, dims=(((1,), (0,)), ((), ()))):
    return dot(a, b, dims).astype(jnp.bfloat16)


def softmax_of(queries, key_rows):
    scores = dot(queries, key_rows, ONES) * DK ** (-0.5)
    exponent = jnp.exp(scores - jnp.max(scores, axis=-1, keepdims=True))
    return exponent * (1.0 / jnp.sum(exponent, axis=-1, keepdims=True))


def forward_kernel(rows, gain, wq, wk, wv, wo, part, normed, total):
    step = pl.program_id(0)

    @pl.when(step == 0)
    def _():
        normed[...] = normalize(rows[...], gain[...])[0]
        total[...] = jnp.zeros_like(total)

    n = normed[...]
    queries, key_rows, value_rows = low_dot(n, wq[...]), low_dot(n, wk[...]), low_dot(n, wv[...])
    parts = []
    for start in range(0, queries.shape[1], DK):
        head = slice(start, start + DK)
        soft = softmax_of(queries[:, head], key_rows[:, head]).astype(jnp.bfloat16)
        parts.append(low_dot(soft, value_rows[:, head]))
    total[...] += dot(jnp.concatenate(parts, axis=1), wo[...])

    @pl.when(step == pl.num_programs(0) - 1)
    def _():
        part[...] = total[...].astype(part.dtype)


def backward_kernel(
    rows, upstream, gain, wq, wk, wv, wo, part, normed, ctx, qg, kg, vg, total
):
    step = pl.program_id(0)

    @pl.when(step == 0)
    def _():
        normed[...] = normalize(rows[...], gain[...])[0]
        total[...] = jnp.zeros_like(total)

    n = normed[...]
    queries, key_rows, value_rows = low_dot(n, wq[...]), low_dot(n, wk[...]), low_dot(n, wv[...])
    ctx_grad = low_dot(upstream[...], wo[...], ONES)
    for start in range(0, queries.shape[1], DK):
        head = slice(start, start + DK)
        q, k, v, c = queries[:, head], key_rows[:, head], value_rows[:, head], ctx_grad[:, head]
        soft = softmax_of(q, k)
        soft_low = soft.astype(jnp.bfloat16)
        ctx[:, head] = low_dot(soft_low, v)
        soft_grad = dot(c, v, ONES)
        vg[:, head] = low_dot(soft_low, c, ZEROS)
        inner = jnp.sum(soft * soft_grad, axis=-1, keepdims=True)
        score_grad = (soft * (soft_grad - inner) * DK ** (-0.5)).astype(jnp.bfloat16)
        qg[:, head] = low_dot(score_grad, k)
        kg[:, head] = low_dot(score_grad, q, ZEROS)
    total[...] += (
        dot(qg[...], wq[...], ONES) + dot(kg[...], wk[...], ONES) + dot(vg[...], wv[...], ONES)
    )

    @pl.when(step == pl.num_programs(0) - 1)
    def _():
        part[...] = total[...].astype(part.dtype)


def gradient_kernel(
    n0, n1, g0, g1, c0, c1, q0, q1, k0, k1, v0, v1, wq, wk, wv, wo, turned, upstream
):
    @pl.when(pl.program_id(0) == 0)
    def _():
        count = n0.shape[0]
        turned[:, :count] = n0[...].T
        turned[:, count:] = n1[...].T
        upstream[:count] = g0[...]
        upstream[count:] = g1[...]

    def both(first, second):
        return jnp.concatenate([first[...], second[...]], axis=0)

    wq[...] = low_dot(turned[...], both(q0, q1))
    wk[...] = low_dot(turned[...], both(k0, k1))
    wv[...] = low_dot(turned[...], both(v0, v1))
    wo[...] = low_dot(both(c0, c1), upstream[...], ZEROS)


def whole(shape):
    return pl.BlockSpec(shape, lambda i: (0,) * len(shape))


def columns(rows, width):
    return pl.BlockSpec((rows, width), lambda i: (0, i))


def row_blocks(width, columns_):
    return pl.BlockSpec((width, columns_), lambda i: (i, 0))


PARAMS = dict(dimension_semantics=("arbitrary",), vmem_limit_bytes=56 * 2**20)


def weight_specs(depth, width):
    return [columns(depth, width)] * 3 + [row_blocks(width, depth)]


def step_width(inner):
    return 4 * DK if inner % (4 * DK) == 0 else DK


def forward_part(rows, weights):
    count, depth = rows.shape
    inner = weights[1].shape[1]
    width = step_width(inner)
    return pl.pallas_call(
        forward_kernel,
        grid=(inner // width,),
        in_specs=[whole((count, depth)), whole((1, depth))] + weight_specs(depth, width),
        out_specs=whole((count, depth)),
        out_shape=jax.ShapeDtypeStruct((count, depth), jnp.bfloat16),
        scratch_shapes=[
            pltpu.VMEM((count, depth), jnp.bfloat16),
            pltpu.VMEM((count, depth), jnp.float32),
        ],
        compiler_params=pltpu.CompilerParams(**PARAMS),
        cost_estimate=pl.CostEstimate(
            flops=8 * count * depth * inner + 4 * count * count * inner,
            bytes_accessed=8 * depth * inner,
            transcendentals=count * count * inner // DK,
        ),
    )(rows, *weights)


def backward_part(rows, upstream, weights):
    count, depth = rows.shape
    inner = weights[1].shape[1]
    width = step_width(inner)
    wide = jax.ShapeDtypeStruct((count, inner), jnp.bfloat16)
    return pl.pallas_call(
        backward_kernel,
        grid=(inner // width,),
        in_specs=[whole((count, depth)), whole((count, depth)), whole((1, depth))]
        + weight_specs(depth, width),
        out_specs=[whole((count, depth)), whole((count, depth))] + [columns(count, width)] * 4,
        out_shape=[
            jax.ShapeDtypeStruct((count, depth), jnp.bfloat16),
            jax.ShapeDtypeStruct((count, depth), jnp.bfloat16),
        ]
        + [wide] * 4,
        scratch_shapes=[pltpu.VMEM((count, depth), jnp.float32)],
        compiler_params=pltpu.CompilerParams(**PARAMS),
        cost_estimate=pl.CostEstimate(
            flops=14 * count * depth * inner + 12 * count * count * inner,
            bytes_accessed=8 * depth * inner,
            transcendentals=count * count * inner // DK,
        ),
    )(rows, upstream, *weights)


def gradients(first, second, g0, g1):
    n0, c0, q0, k0, v0 = first
    n1, c1, q1, k1, v1 = second
    count, depth = n0.shape
    inner = q0.shape[1]
    width = step_width(inner)
    low = jnp.bfloat16
    return pl.pallas_call(
        gradient_kernel,
        grid=(inner // width,),
        in_specs=[whole((count, depth))] * 4 + [columns(count, width)] * 8,
        out_specs=weight_specs(depth, width),
        out_shape=[jax.ShapeDtypeStruct((depth, inner), low)] * 3
        + [jax.ShapeDtypeStruct((inner, depth), low)],
        scratch_shapes=[
            pltpu.VMEM((depth, 2 * count), low),
            pltpu.VMEM((2 * count, depth), low),
        ],
        compiler_params=pltpu.CompilerParams(**PARAMS),
        cost_estimate=pl.CostEstimate(
            flops=16 * count * depth * inner, bytes_accessed=8 * depth * inner, transcendentals=0
        ),
    )(n0, n1, g0, g1, c0, c1, q0, q1, k0, k1, v0, v1)


def relay_kernel(
    heads, sections, last, x, b, g, gain, fpart, bpart, before,
    x_next, g_next, gain_out, landed, hop, gains, gains_in, sent, got, hop_sent, hop_got
):
    me, section = lax.axis_index("head"), lax.axis_index("section")
    ahead = lax.rem(section + 1, sections)
    back = lax.rem(section + sections - 1, sections)
    share = x.shape[0] // heads
    peers = [lax.rem(me + d, heads) for d in range(1, heads)]

    barrier = pltpu.get_barrier_semaphore()
    for peer in peers:
        pl.semaphore_signal(barrier, inc=1, device_id={"head": peer})
    for other in (ahead, back):
        pl.semaphore_signal(barrier, inc=1, device_id={"section": other})
    pl.semaphore_wait(barrier, heads + 1)

    def rows_of(index):
        return pl.ds(pl.multiple_of(index * share, share), share)

    def sending(source, target, slot, d, where):
        return pltpu.make_async_remote_copy(
            src_ref=source,
            dst_ref=target,
            send_sem=sent.at[slot, d],
            recv_sem=got.at[slot, d],
            device_id=where,
            device_id_type=pl.DeviceIdType.MESH,
        )

    own = rows_of(me)
    scattered = [
        [
            sending(part.at[rows_of(peer)], landed.at[chain, d], chain, d, {"head": peer})
            for d, peer in enumerate(peers)
        ]
        for chain, part in enumerate((fpart, bpart))
    ]
    for copies in scattered:
        for copy in copies:
            copy.start()

    def summed(chain, part):
        for copy in scattered[chain]:
            copy.wait()
        total = part[own, :].astype(jnp.float32)
        for d in range(heads - 1):
            total += landed[chain, d].astype(jnp.float32)
        return total

    def hopping(chain, target, where):
        return pltpu.make_async_remote_copy(
            src_ref=hop.at[chain],
            dst_ref=target.at[own],
            send_sem=hop_sent.at[chain],
            recv_sem=hop_got.at[chain],
            device_id={"section": where},
            device_id_type=pl.DeviceIdType.MESH,
        )

    hop[0] = (x[own, :].astype(jnp.float32) + summed(0, fpart)).astype(hop.dtype)
    forward_hop = hopping(0, x_next, ahead)
    forward_hop.start()

    normed_grad = summed(1, bpart)
    normed, unit_rows, inverse = normalize(b[own, :], gain[...])
    unit_grad = normed_grad * gain[...]
    along = jnp.mean(unit_grad * unit_rows, axis=-1, keepdims=True)
    returned = g[own, :].astype(jnp.float32) + inverse * (unit_grad - unit_rows * along)
    hop[1] = returned.astype(hop.dtype)
    backward_hop = hopping(1, g_next, back)
    backward_hop.start()

    products = normed_grad * unit_rows
    gain_sum = before[...]
    for start in range(0, share, 8):
        gain_sum += products[start : start + 8]
    gathers = []
    if last:
        gains[...] = gain_sum
        for d, peer in enumerate(peers):
            gathers.append(sending(gains, gains_in.at[d], 4, d, {"head": peer}))
            gathers[-1].start()
    for chain, (copy, block) in enumerate(((forward_hop, x_next), (backward_hop, g_next))):
        copy.wait()
        for d, peer in enumerate(peers):
            gathers.append(sending(block.at[own], block.at[own], 2 + chain, d, {"head": peer}))
            gathers[-1].start()
    for copy in gathers:
        copy.wait()
    if last:
        for d in range(heads - 1):
            gain_sum += gains_in[d]
    gain_out[...] = gain_sum


def relay(x, b, g, gain, fpart, bpart, before, last):
    heads, sections = lax.axis_size("head"), lax.axis_size("section")
    count, depth = x.shape
    share = count // heads
    low = jnp.bfloat16
    in_vmem = pl.BlockSpec(memory_space=pltpu.VMEM)
    dma = pltpu.SemaphoreType.DMA
    return pl.pallas_call(
        functools.partial(relay_kernel, heads, sections, last),
        in_specs=[in_vmem] * 7,
        out_specs=[in_vmem] * 3,
        out_shape=[
            jax.ShapeDtypeStruct((count, depth), low),
            jax.ShapeDtypeStruct((count, depth), low),
            jax.ShapeDtypeStruct((8, depth), jnp.float32),
        ],
        scratch_shapes=[
            pltpu.VMEM((2, heads - 1, share, depth), low),
            pltpu.VMEM((2, share, depth), low),
            pltpu.VMEM((8, depth), jnp.float32),
            pltpu.VMEM((heads - 1, 8, depth), jnp.float32),
            dma((5, heads - 1)),
            dma((5, heads - 1)),
            dma((2,)),
            dma((2,)),
        ],
        compiler_params=pltpu.CompilerParams(
            collective_id=int(last), has_side_effects=True, vmem_limit_bytes=24 * 2**20
        ),
    )(x, b, g, gain, fpart, bpart, before)


def per_device(
    section_inputs,
    section_cotangents,
    fresh_tokens,
    fresh_cotangents,
    norm_gain,
    query_weight,
    key_weight,
    value_weight,
    out_weight,
    saved_inputs,
    reload_slot,
):
    section_count = lax.axis_size("section")
    section_index = lax.axis_index("section")
    head_index = lax.axis_index("head")
    mirror_index = section_count - 1 - section_index
    share_width = saved_inputs.shape[3]
    column_start = head_index * share_width
    weights = (norm_gain, query_weight[0], key_weight[0], value_weight[0], out_weight[0])
    x0 = section_inputs[0]
    g0 = section_cotangents[0]
    store = saved_inputs[0]
    count = x0.shape[0]

    def own_share(block):
        return lax.dynamic_slice_in_dim(block, column_start, share_width, 1)

    held = lax.dynamic_index_in_dim(reload_slot, mirror_index, 1, keepdims=False)
    held0 = lax.dynamic_index_in_dim(store, held[0], 0, keepdims=False)
    held1 = lax.dynamic_index_in_dim(store, held[1], 0, keepdims=False)
    own = lax.dynamic_index_in_dim(reload_slot, section_index, 1, keepdims=False)

    travel = mirrored(jnp.concatenate([own_share(x0), held0, held1], axis=0), "section")
    arrived, reloads = travel[:count], travel[count:]
    restored = lax.all_gather(reloads, "head", axis=1, tiled=True)
    b0 = restored[:count]
    b1 = jnp.where(own[0] == own[1], x0, restored[count:])

    first_section = section_index == 0
    last_section = section_index == section_count - 1
    forward0 = forward_part(x0, weights)
    back0, *first = backward_part(b0, g0, weights)
    nothing = jnp.zeros((8, x0.shape[1]), jnp.float32)
    made, returned, gain0 = relay(x0, b0, g0, norm_gain, forward0, back0, nothing, False)
    x1 = jnp.where(first_section, fresh_tokens[0], made)
    g1 = jnp.where(last_section, fresh_cotangents[0], returned)

    arrived1 = mirrored(own_share(x1), "section")
    store = lax.dynamic_update_index_in_dim(store, arrived, held[0], 0)
    store = lax.dynamic_update_index_in_dim(store, arrived1, held[1], 0)
    forward1 = forward_part(x1, weights)
    back1, *second = backward_part(b1, g1, weights)
    made, returned, gain1 = relay(x1, b1, g1, norm_gain, forward1, back1, gain0, True)
    x2 = jnp.where(first_section, fresh_tokens[1], made)
    g2 = jnp.where(last_section, fresh_cotangents[1], returned)

    grads = gradients(first, second, g0, g1)
    gain = lax.dynamic_slice_in_dim(jnp.sum(gain1, axis=0), column_start, share_width, 0)
    return (x2[None], g2[None], store[None], *(grad[None] for grad in grads), gain[None])


def solution(mesh):
    placed = (
        P("section", None, None),
        P("section", None, None),
        P(),
        P(),
        P("section", None),
        P("section", None, "head"),
        P("section", None, "head"),
        P("section", None, "head"),
        P("section", "head", None),
        P("section", None, None, "head"),
        P(),
    )
    return jax.shard_map(
        per_device,
        mesh=mesh,
        in_specs=placed,
        out_specs=(
            P("section", None, None),
            P("section", None, None),
            P("section", None, None, "head"),
            P("section", None, "head"),
            P("section", None, "head"),
            P("section", None, "head"),
            P("section", "head", None),
            P("section", "head"),
        ),
        check_vma=False,
    )
```

```python
import functools

import jax
import jax.numpy as jnp
from jax import lax
from jax.experimental import pallas as pl
from jax.experimental.pallas import tpu as pltpu
from jax.sharding import PartitionSpec as P

DK = 128
TICKS = 2


epsilon = 1e-06
ONES = (((1,), (1,)), ((), ()))
ZEROS = (((0,), (0,)), ((), ()))


def mirrored(value, axis):
    count = lax.axis_size(axis)
    return lax.ppermute(value, axis, [(i, count - 1 - i) for i in range(count)])


def normalize(rows, gain_row):
    floats = rows.astype(jnp.float32)
    inverse = lax.rsqrt(jnp.mean(floats * floats, axis=-1, keepdims=True) + epsilon)
    unit_rows = floats * inverse
    return ((unit_rows * gain_row).astype(jnp.bfloat16), unit_rows, inverse)


def dot(a, b, dims=(((1,), (0,)), ((), ()))):
    return lax.dot_general(a, b, dims, preferred_element_type=jnp.float32)


def low_dot(a, b, dims=(((1,), (0,)), ((), ()))):
    return dot(a, b, dims).astype(jnp.bfloat16)


def softmax_of(queries, key_rows):
    scores = dot(queries, key_rows, ONES) * DK ** (-0.5)
    exponent = jnp.exp(scores - jnp.max(scores, axis=-1, keepdims=True))
    return exponent * (1.0 / jnp.sum(exponent, axis=-1, keepdims=True))


def forward_kernel(rows, gain, wq, wk, wv, wo, part, normed, total):
    step = pl.program_id(0)

    @pl.when(step == 0)
    def _():
        normed[...] = normalize(rows[...], gain[...])[0]
        total[...] = jnp.zeros_like(total)

    n = normed[...]
    queries, key_rows, value_rows = low_dot(n, wq[...]), low_dot(n, wk[...]), low_dot(n, wv[...])
    parts = []
    for start in range(0, queries.shape[1], DK):
        head = slice(start, start + DK)
        soft = softmax_of(queries[:, head], key_rows[:, head]).astype(jnp.bfloat16)
        parts.append(low_dot(soft, value_rows[:, head]))
    total[...] += dot(jnp.concatenate(parts, axis=1), wo[...])

    @pl.when(step == pl.num_programs(0) - 1)
    def _():
        part[...] = total[...].astype(part.dtype)


def backward_kernel(
    rows, upstream, gain, wq, wk, wv, wo, part, normed, ctx, qg, kg, vg, total
):
    step = pl.program_id(0)

    @pl.when(step == 0)
    def _():
        normed[...] = normalize(rows[...], gain[...])[0]
        total[...] = jnp.zeros_like(total)

    n = normed[...]
    queries, key_rows, value_rows = low_dot(n, wq[...]), low_dot(n, wk[...]), low_dot(n, wv[...])
    ctx_grad = low_dot(upstream[...], wo[...], ONES)
    for start in range(0, queries.shape[1], DK):
        head = slice(start, start + DK)
        q, k, v, c = queries[:, head], key_rows[:, head], value_rows[:, head], ctx_grad[:, head]
        soft = softmax_of(q, k)
        soft_low = soft.astype(jnp.bfloat16)
        ctx[:, head] = low_dot(soft_low, v)
        soft_grad = dot(c, v, ONES)
        vg[:, head] = low_dot(soft_low, c, ZEROS)
        inner = jnp.sum(soft * soft_grad, axis=-1, keepdims=True)
        score_grad = (soft * (soft_grad - inner) * DK ** (-0.5)).astype(jnp.bfloat16)
        qg[:, head] = low_dot(score_grad, k)
        kg[:, head] = low_dot(score_grad, q, ZEROS)
    total[...] += (
        dot(qg[...], wq[...], ONES) + dot(kg[...], wk[...], ONES) + dot(vg[...], wv[...], ONES)
    )

    @pl.when(step == pl.num_programs(0) - 1)
    def _():
        part[...] = total[...].astype(part.dtype)


def gradient_kernel(
    n0, n1, g0, g1, c0, c1, q0, q1, k0, k1, v0, v1, wq, wk, wv, wo, turned, upstream
):
    @pl.when(pl.program_id(0) == 0)
    def _():
        count = n0.shape[0]
        turned[:, :count] = n0[...].T
        turned[:, count:] = n1[...].T
        upstream[:count] = g0[...]
        upstream[count:] = g1[...]

    def both(first, second):
        return jnp.concatenate([first[...], second[...]], axis=0)

    wq[...] = low_dot(turned[...], both(q0, q1))
    wk[...] = low_dot(turned[...], both(k0, k1))
    wv[...] = low_dot(turned[...], both(v0, v1))
    wo[...] = low_dot(both(c0, c1), upstream[...], ZEROS)


def whole(shape):
    return pl.BlockSpec(shape, lambda i: (0,) * len(shape))


def columns(rows, width):
    return pl.BlockSpec((rows, width), lambda i: (0, i))


def row_blocks(width, columns_):
    return pl.BlockSpec((width, columns_), lambda i: (i, 0))


PARAMS = dict(dimension_semantics=("arbitrary",), vmem_limit_bytes=56 * 2**20)


def weight_specs(depth, width):
    return [columns(depth, width)] * 3 + [row_blocks(width, depth)]


def step_width(inner):
    return 4 * DK if inner % (4 * DK) == 0 else DK


def forward_part(rows, weights):
    count, depth = rows.shape
    inner = weights[1].shape[1]
    width = step_width(inner)
    return pl.pallas_call(
        forward_kernel,
        grid=(inner // width,),
        in_specs=[whole((count, depth)), whole((1, depth))] + weight_specs(depth, width),
        out_specs=whole((count, depth)),
        out_shape=jax.ShapeDtypeStruct((count, depth), jnp.bfloat16),
        scratch_shapes=[
            pltpu.VMEM((count, depth), jnp.bfloat16),
            pltpu.VMEM((count, depth), jnp.float32),
        ],
        compiler_params=pltpu.CompilerParams(**PARAMS),
        cost_estimate=pl.CostEstimate(
            flops=8 * count * depth * inner + 4 * count * count * inner,
            bytes_accessed=8 * depth * inner,
            transcendentals=count * count * inner // DK,
        ),
    )(rows, *weights)


def backward_part(rows, upstream, weights):
    count, depth = rows.shape
    inner = weights[1].shape[1]
    width = step_width(inner)
    wide = jax.ShapeDtypeStruct((count, inner), jnp.bfloat16)
    return pl.pallas_call(
        backward_kernel,
        grid=(inner // width,),
        in_specs=[whole((count, depth)), whole((count, depth)), whole((1, depth))]
        + weight_specs(depth, width),
        out_specs=[whole((count, depth)), whole((count, depth))] + [columns(count, width)] * 4,
        out_shape=[
            jax.ShapeDtypeStruct((count, depth), jnp.bfloat16),
            jax.ShapeDtypeStruct((count, depth), jnp.bfloat16),
        ]
        + [wide] * 4,
        scratch_shapes=[pltpu.VMEM((count, depth), jnp.float32)],
        compiler_params=pltpu.CompilerParams(**PARAMS),
        cost_estimate=pl.CostEstimate(
            flops=14 * count * depth * inner + 12 * count * count * inner,
            bytes_accessed=8 * depth * inner,
            transcendentals=count * count * inner // DK,
        ),
    )(rows, upstream, *weights)


def gradients(first, second, g0, g1):
    n0, c0, q0, k0, v0 = first
    n1, c1, q1, k1, v1 = second
    count, depth = n0.shape
    inner = q0.shape[1]
    width = step_width(inner)
    low = jnp.bfloat16
    return pl.pallas_call(
        gradient_kernel,
        grid=(inner // width,),
        in_specs=[whole((count, depth))] * 4 + [columns(count, width)] * 8,
        out_specs=weight_specs(depth, width),
        out_shape=[jax.ShapeDtypeStruct((depth, inner), low)] * 3
        + [jax.ShapeDtypeStruct((inner, depth), low)],
        scratch_shapes=[
            pltpu.VMEM((depth, 2 * count), low),
            pltpu.VMEM((2 * count, depth), low),
        ],
        compiler_params=pltpu.CompilerParams(**PARAMS),
        cost_estimate=pl.CostEstimate(
            flops=16 * count * depth * inner, bytes_accessed=8 * depth * inner, transcendentals=0
        ),
    )(n0, n1, g0, g1, c0, c1, q0, q1, k0, k1, v0, v1)


def relay_kernel(
    heads, sections, last, x, b, g, gain, fpart, bpart, before,
    x_next, g_next, gain_out, landed, hop, gains, gains_in, sent, got, hop_sent, hop_got
):
    me, section = lax.axis_index("head"), lax.axis_index("section")
    ahead = lax.rem(section + 1, sections)
    back = lax.rem(section + sections - 1, sections)
    share = x.shape[0] // heads
    peers = [lax.rem(me + d, heads) for d in range(1, heads)]

    barrier = pltpu.get_barrier_semaphore()
    for peer in peers:
        pl.semaphore_signal(barrier, inc=1, device_id={"head": peer})
    for other in (ahead, back):
        pl.semaphore_signal(barrier, inc=1, device_id={"section": other})
    pl.semaphore_wait(barrier, heads + 1)

    def rows_of(index):
        return pl.ds(pl.multiple_of(index * share, share), share)

    def sending(source, target, slot, d, where):
        return pltpu.make_async_remote_copy(
            src_ref=source,
            dst_ref=target,
            send_sem=sent.at[slot, d],
            recv_sem=got.at[slot, d],
            device_id=where,
            device_id_type=pl.DeviceIdType.MESH,
        )

    own = rows_of(me)
    scattered = [
        [
            sending(part.at[rows_of(peer)], landed.at[chain, d], chain, d, {"head": peer})
            for d, peer in enumerate(peers)
        ]
        for chain, part in enumerate((fpart, bpart))
    ]
    for copies in scattered:
        for copy in copies:
            copy.start()

    def summed(chain, part):
        for copy in scattered[chain]:
            copy.wait()
        total = part[own, :].astype(jnp.float32)
        for d in range(heads - 1):
            total += landed[chain, d].astype(jnp.float32)
        return total

    def hopping(chain, target, where):
        return pltpu.make_async_remote_copy(
            src_ref=hop.at[chain],
            dst_ref=target.at[own],
            send_sem=hop_sent.at[chain],
            recv_sem=hop_got.at[chain],
            device_id={"section": where},
            device_id_type=pl.DeviceIdType.MESH,
        )

    hop[0] = (x[own, :].astype(jnp.float32) + summed(0, fpart)).astype(hop.dtype)
    forward_hop = hopping(0, x_next, ahead)
    forward_hop.start()

    normed_grad = summed(1, bpart)
    normed, unit_rows, inverse = normalize(b[own, :], gain[...])
    unit_grad = normed_grad * gain[...]
    along = jnp.mean(unit_grad * unit_rows, axis=-1, keepdims=True)
    returned = g[own, :].astype(jnp.float32) + inverse * (unit_grad - unit_rows * along)
    hop[1] = returned.astype(hop.dtype)
    backward_hop = hopping(1, g_next, back)
    backward_hop.start()

    products = normed_grad * unit_rows
    gain_sum = before[...]
    for start in range(0, share, 8):
        gain_sum += products[start : start + 8]
    gathers = []
    if last:
        gains[...] = gain_sum
        for d, peer in enumerate(peers):
            gathers.append(sending(gains, gains_in.at[d], 4, d, {"head": peer}))
            gathers[-1].start()
    for chain, (copy, block) in enumerate(((forward_hop, x_next), (backward_hop, g_next))):
        copy.wait()
        for d, peer in enumerate(peers):
            gathers.append(sending(block.at[own], block.at[own], 2 + chain, d, {"head": peer}))
            gathers[-1].start()
    for copy in gathers:
        copy.wait()
    if last:
        for d in range(heads - 1):
            gain_sum += gains_in[d]
    gain_out[...] = gain_sum


def relay(x, b, g, gain, fpart, bpart, before, last):
    heads, sections = lax.axis_size("head"), lax.axis_size("section")
    count, depth = x.shape
    share = count // heads
    low = jnp.bfloat16
    in_vmem = pl.BlockSpec(memory_space=pltpu.VMEM)
    dma = pltpu.SemaphoreType.DMA
    return pl.pallas_call(
        functools.partial(relay_kernel, heads, sections, last),
        in_specs=[in_vmem] * 7,
        out_specs=[in_vmem] * 3,
        out_shape=[
            jax.ShapeDtypeStruct((count, depth), low),
            jax.ShapeDtypeStruct((count, depth), low),
            jax.ShapeDtypeStruct((8, depth), jnp.float32),
        ],
        scratch_shapes=[
            pltpu.VMEM((2, heads - 1, share, depth), low),
            pltpu.VMEM((2, share, depth), low),
            pltpu.VMEM((8, depth), jnp.float32),
            pltpu.VMEM((heads - 1, 8, depth), jnp.float32),
            dma((5, heads - 1)),
            dma((5, heads - 1)),
            dma((2,)),
            dma((2,)),
        ],
        compiler_params=pltpu.CompilerParams(
            collective_id=int(last), has_side_effects=True, vmem_limit_bytes=24 * 2**20
        ),
    )(x, b, g, gain, fpart, bpart, before)


def per_device(
    section_inputs,
    section_cotangents,
    fresh_tokens,
    fresh_cotangents,
    norm_gain,
    query_weight,
    key_weight,
    value_weight,
    out_weight,
    saved_inputs,
    reload_slot,
):
    section_count = lax.axis_size("section")
    section_index = lax.axis_index("section")
    head_index = lax.axis_index("head")
    mirror_index = section_count - 1 - section_index
    share_width = saved_inputs.shape[3]
    column_start = head_index * share_width
    weights = (norm_gain, query_weight[0], key_weight[0], value_weight[0], out_weight[0])
    x0 = section_inputs[0]
    g0 = section_cotangents[0]
    store = saved_inputs[0]
    count = x0.shape[0]

    def own_share(block):
        return lax.dynamic_slice_in_dim(block, column_start, share_width, 1)

    held = lax.dynamic_index_in_dim(reload_slot, mirror_index, 1, keepdims=False)
    held0 = lax.dynamic_index_in_dim(store, held[0], 0, keepdims=False)
    held1 = lax.dynamic_index_in_dim(store, held[1], 0, keepdims=False)
    own = lax.dynamic_index_in_dim(reload_slot, section_index, 1, keepdims=False)

    travel = mirrored(jnp.concatenate([own_share(x0), held0, held1], axis=0), "section")
    arrived, reloads = travel[:count], travel[count:]
    b0 = lax.all_gather(reloads[:count], "head", axis=1, tiled=True)

    first_section = section_index == 0
    last_section = section_index == section_count - 1
    forward0 = forward_part(x0, weights)
    later, forward0 = lax.optimization_barrier((reloads[count:], forward0))
    restored = lax.all_gather(later, "head", axis=1, tiled=True)
    b1 = jnp.where(own[0] == own[1], x0, restored)
    back0, *first = backward_part(b0, g0, weights)
    nothing = jnp.zeros((8, x0.shape[1]), jnp.float32)
    made, returned, gain0 = relay(x0, b0, g0, norm_gain, forward0, back0, nothing, False)
    x1 = jnp.where(first_section, fresh_tokens[0], made)
    g1 = jnp.where(last_section, fresh_cotangents[0], returned)

    arrived1 = mirrored(own_share(x1), "section")
    store = lax.dynamic_update_index_in_dim(store, arrived, held[0], 0)
    store = lax.dynamic_update_index_in_dim(store, arrived1, held[1], 0)
    forward1 = forward_part(x1, weights)
    back1, *second = backward_part(b1, g1, weights)
    made, returned, gain1 = relay(x1, b1, g1, norm_gain, forward1, back1, gain0, True)
    x2 = jnp.where(first_section, fresh_tokens[1], made)
    g2 = jnp.where(last_section, fresh_cotangents[1], returned)

    grads = gradients(first, second, g0, g1)
    gain = lax.dynamic_slice_in_dim(jnp.sum(gain1, axis=0), column_start, share_width, 0)
    return (x2[None], g2[None], store[None], *(grad[None] for grad in grads), gain[None])


def solution(mesh):
    placed = (
        P("section", None, None),
        P("section", None, None),
        P(),
        P(),
        P("section", None),
        P("section", None, "head"),
        P("section", None, "head"),
        P("section", None, "head"),
        P("section", "head", None),
        P("section", None, None, "head"),
        P(),
    )
    return jax.shard_map(
        per_device,
        mesh=mesh,
        in_specs=placed,
        out_specs=(
            P("section", None, None),
            P("section", None, None),
            P("section", None, None, "head"),
            P("section", None, "head"),
            P("section", None, "head"),
            P("section", None, "head"),
            P("section", "head", None),
            P("section", "head"),
        ),
        check_vma=False,
    )
```
